32 devices in a mesh: group: 2 (over y), phi: 4 (over z), eta: 2 (over x), half: 2 (over core).
Axes of the slice: x: 2, y: 2, z: 4, core: 2. Of those that a mesh axis runs over, the one named last changes fastest.
Arguments:
- feats: bfloat16 [8, 2, 512, 512], P(('group', 'phi'), 'eta', 'half'), parts along dimension 0, may hold values from -6 to 6
- cotangent: bfloat16 [8, 2, 512, 512], P(('group', 'phi'), 'eta', 'half'), parts along dimension 0, may hold values from -6 to 6
- tiles: bfloat16 [8, 2, 24, 128, 128], P(('group', 'phi'), 'eta', 'half'), parts along dimension 0, may hold values from -0.21875 to 0.21875
- tile_src: int32 [8, 2, 24], P(('group', 'phi'), 'eta', 'half'), parts along dimension 0, may hold values from 0 to 5
- tile_dst: int32 [8, 2, 24], P(('group', 'phi'), 'eta', 'half'), parts along dimension 0, may hold values from -1 to 3, as said below
- weights: bfloat16 [2, 512, 512], replicated, may hold values from -0.25 to 0.25
- mask: int32 [2, 8, 8], replicated, may hold values 0 or 1
- counts: int32 [8, 2], P(('group', 'phi'), 'eta'), parts along dimension 0, may hold values from 128 to 512, as said below
Outputs:
- final: bfloat16 [8, 2, 512, 512], P(('group', 'phi'), 'eta', 'half'), parts along dimension 0
- grad_w: float32 [4, 512, 512], P('group', 'phi'), parts along dimension 0
The draws below stay inside these ranges and needn't reach their ends.
There are 2 independent parts, one for each index of `group`. The reference program is written for one: setup_inputs(seed, part) draws one part's arguments, and reference() takes and returns one part's arrays. A program takes and returns all parts, laid end to end along the dimension named above; an argument that names none is the same for every part. Nothing has to cross between parts.
Inputs may be any that keep to these rules, and one draw needn't show every extreme that they name: `tile_dst`: in each region half the live tiles fill the first slots and the rest hold -1; some region half has all 12 slots live. `counts`: some region is full and some holds a quarter of its hits.
All inputs are finite; a program needn't handle non-finite values.
Results may differ from the reference program's by a relative error of at most 0.017.
Values may be sent and summed in bfloat16 or wider, within the bound.
No kernel may reach another device: no remote copies, remote signals or barrier semaphores. Data moves between devices by JAX's collectives and lax.ppermute only.
A program may use at most 64 MiB of HBM per device.

```python
import jax
import jax.numpy as jnp
from jax import lax

D = 512
MB = 8
BLOCK = 128
HB = 2
NT = 12
LAYERS = 2
PHI_REG = 4
ETA_REG = 2
HALVES = 2
REG_BLOCKS = 4
SLOTS = 6


def draw_tile_dst(key, part):
    key_level = jax.random.fold_in(key, 11)
    key_full = jax.random.fold_in(key, 12)
    key_target = jax.random.fold_in(key, 13)
    shape_dev = (PHI_REG, ETA_REG, HALVES)
    level = jax.random.randint(key_level, shape_dev, 0, 4)
    live = NT // jnp.left_shift(jnp.ones(shape_dev, jnp.int32), level)
    live = jnp.maximum(live, 1)
    full = jax.random.randint(key_full, (), 0, PHI_REG * ETA_REG * HALVES)
    places = jnp.arange(PHI_REG * ETA_REG * HALVES, dtype=jnp.int32).reshape(shape_dev)
    live = jnp.where(places == full, NT, live)
    targets = jax.random.randint(key_target, shape_dev + (NT,), 0, REG_BLOCKS)
    slot = jnp.arange(NT, dtype=jnp.int32)
    result = jnp.where(slot < live[..., None], targets, -1)
    return result.reshape(PHI_REG, ETA_REG, HALVES * NT).astype(jnp.int32)


def draw_counts(key, part):
    key_vals = jax.random.fold_in(key, 21)
    key_full = jax.random.fold_in(key, 22)
    total = REG_BLOCKS * BLOCK
    regions = PHI_REG * ETA_REG
    values = jax.random.randint(key_vals, (regions,), total // 4, total + 1)
    full = jax.random.randint(key_full, (), 0, regions)
    places = jnp.arange(regions, dtype=jnp.int32)
    values = jnp.where(places == full, total, values)
    values = jnp.where(places == (full + 1) % regions, total // 4, values)
    return values.reshape(PHI_REG, ETA_REG).astype(jnp.int32)


def touch_ends(drawn, rng, low, largest):
    spot = [jax.random.randint(jax.random.fold_in(rng, axis), (), 0, length) for axis, length in enumerate(drawn.shape)]
    widest = drawn.shape.index(max(drawn.shape))
    neighbour = spot[:widest] + [(spot[widest] + 1) % drawn.shape[widest]] + spot[widest + 1:]
    return drawn.at[tuple(spot)].set(low).at[tuple(neighbour)].set(largest)


def level_of(own_key, extent, shards, smallest, high):
    loudness, own = 1.0, jax.random.fold_in(own_key, 6)
    for dim, shards_of in shards:
        steps = jnp.exp(jax.random.uniform(jax.random.fold_in(own, dim), (shards_of,), jnp.float32, smallest / len(shards), high / len(shards)))
        loudness = loudness * jnp.repeat(steps, extent[dim] // shards_of).reshape([-1 if axis == dim else 1 for axis in range(len(extent))])
    return loudness


def bell_draw(key, dims, scale, bound, split=(), held_as=jnp.bfloat16):
    factor_of = level_of(key, dims, split, -0.22, 0.18) if split else 1.0
    values = jax.random.normal(key, dims, jnp.float32) * scale * factor_of
    return jnp.minimum(jnp.maximum(values, -bound), bound).astype(held_as)


def setup_inputs(seed: int = 0, part: int = 0) -> dict:
    seeds = jax.random.split(jax.random.key(seed), 9)
    part_splits = jax.random.split(jax.random.fold_in(seeds[8], part), 9)
    return {
        "feats": bell_draw(part_splits[0], (PHI_REG, ETA_REG, REG_BLOCKS * BLOCK, D), 1.0, 6.0, ((0, 4), (1, 2), (2, 2))),
        "cotangent": bell_draw(part_splits[1], (PHI_REG, ETA_REG, REG_BLOCKS * BLOCK, D), 1.0, 6.0, ((0, 4), (1, 2), (2, 2))),
        "tiles": bell_draw(part_splits[2], (PHI_REG, ETA_REG, HALVES * NT, BLOCK, BLOCK), (BLOCK * NT // HB) ** -0.5, 0.21875, ((0, 4), (1, 2), (2, 2))),
        "tile_src": touch_ends(jax.random.randint(part_splits[3], (PHI_REG, ETA_REG, HALVES * NT), 0, SLOTS), jax.random.fold_in(part_splits[3], 1), 0, SLOTS - 1).astype(jnp.int32),
        "tile_dst": draw_tile_dst(jax.random.fold_in(jax.random.fold_in(seeds[8], part), 71), part),
        "weights": bell_draw(seeds[5], (LAYERS, D, D), D ** -0.5, 0.25),
        "mask": touch_ends((jax.random.randint(seeds[6], (LAYERS, MB, MB), 0, 4) < 3).astype(jnp.int32), jax.random.fold_in(seeds[6], 1), 0, 1),
        "counts": draw_counts(jax.random.fold_in(jax.random.fold_in(seeds[8], part), 71), part),
    }


def silu_slope(pre):
    sigma = jax.nn.sigmoid(pre)
    return sigma * (1.0 + pre * (1.0 - sigma))

def aggregate(hfloat, tiles, tile_src, tile_dst, rounded):
    blocks = hfloat.reshape(PHI_REG, ETA_REG, HALVES, HB, BLOCK, D)
    edge = blocks[:, :, :, 0]
    empty = jnp.zeros_like(edge[:, :1])
    lower_phi = jnp.roll(edge, 1, axis=0)
    upper_phi = jnp.roll(edge, -1, axis=0)
    lower_eta = jnp.concatenate([empty, edge[:, :-1]], axis=1)
    upper_eta = jnp.concatenate([edge[:, 1:], empty], axis=1)
    rims = jnp.stack([lower_phi, upper_phi, lower_eta, upper_eta], axis=3)
    sources = jnp.concatenate([blocks, rims], axis=3).reshape(PHI_REG * ETA_REG, HALVES * SLOTS, BLOCK, D)
    owner = jnp.arange(HALVES * NT, dtype=jnp.int32) // NT * SLOTS
    picks = tile_src.reshape(PHI_REG * ETA_REG, HALVES * NT).astype(jnp.int32) + owner[None, :]
    targets = tile_dst.reshape(PHI_REG * ETA_REG, HALVES * NT).astype(jnp.int32)
    tile_sets = tiles.reshape(PHI_REG * ETA_REG, HALVES * NT, BLOCK, BLOCK)
    block_ids = jnp.arange(REG_BLOCKS, dtype=jnp.int32)

    def region(item):
        source_set, tile_set, pick, target = item
        picked = jnp.take(source_set, pick, axis=0)
        parts = jnp.einsum('tij,tjd->tid', tile_set.astype(jnp.float32), picked, precision=lax.Precision.HIGHEST)
        parts = parts.reshape(HALVES, NT, BLOCK, D)
        target_half = target.reshape(HALVES, NT)
        onehot = (target_half[:, None, :] == block_ids[None, :, None]).astype(hfloat.dtype)
        per_half = jnp.einsum('hbt,htid->hbid', onehot, parts, precision=lax.Precision.HIGHEST)
        if rounded:
            per_half = lax.optimization_barrier(per_half.astype(jnp.bfloat16)).astype(hfloat.dtype)
        return lax.optimization_barrier(jnp.sum(per_half, axis=0))
    summed = lax.map(region, (sources, tile_sets, picks, targets))
    return summed.reshape(PHI_REG, ETA_REG, REG_BLOCKS * BLOCK, D)

def reference(feats, cotangent, tiles, tile_src, tile_dst, weights, mask, counts):
    rows_all = REG_BLOCKS * BLOCK
    live = (jnp.arange(rows_all, dtype=jnp.int32)[None, None, :] < counts[:, :, None]).astype(jnp.float32)[..., None]
    side = D // MB
    mask_full = jnp.broadcast_to(mask[:, :, None, :, None], (LAYERS, MB, side, MB, side)).reshape(LAYERS, D, D).astype(jnp.float32)
    masked = (weights.astype(jnp.float32) * mask_full).astype(jnp.bfloat16)
    state = feats
    inputs = []
    pres = []
    for layer in range(LAYERS):
        hfloat = state.astype(jnp.float32)
        mixed = (hfloat + aggregate(hfloat, tiles, tile_src, tile_dst, True)).astype(jnp.bfloat16)
        pre = jnp.dot(mixed.reshape(-1, D), masked[layer], preferred_element_type=jnp.float32).reshape(mixed.shape)
        state = (live * (hfloat + jax.nn.silu(pre))).astype(jnp.bfloat16)
        inputs.append(mixed)
        pres.append(pre)
    upstream = cotangent.astype(jnp.float32)
    grads = [None] * LAYERS
    for layer in reversed(range(LAYERS)):
        delta = (upstream * live * silu_slope(pres[layer])).astype(jnp.bfloat16)
        flat_delta = delta.reshape(-1, D)
        grads[layer] = jnp.dot(inputs[layer].reshape(-1, D).T, flat_delta, preferred_element_type=jnp.float32) * mask_full[layer]
        if layer > 0:
            back = jnp.dot(flat_delta, masked[layer].T, preferred_element_type=jnp.float32).astype(jnp.bfloat16)
            backf = back.reshape(delta.shape).astype(jnp.float32)
            unused, pullback = jax.vjp(lambda value: aggregate(value, tiles, tile_src, tile_dst, False), jnp.zeros_like(backf))
            spread = pullback(backf)[0]
            upstream = live * upstream + backf + spread
    return (state, jnp.stack(grads))
```

```python
import functools

import jax
import jax.numpy as jnp
from jax import lax
from jax.experimental import pallas as pl
from jax.experimental.pallas import tpu as pltpu
from jax.sharding import PartitionSpec as P

BF16 = jnp.bfloat16
F32 = jnp.float32
VMEM = pl.BlockSpec(memory_space=pltpu.VMEM)
SMEM = pl.BlockSpec(memory_space=pltpu.SMEM)


def call(kernel, ins, outs, scratch=(), flops=0, name=None):
    moved = sum(a.size * a.dtype.itemsize for a in ins)
    moved += sum(a.size * a.dtype.itemsize for a in outs)
    return pl.pallas_call(
        kernel,
        out_shape=outs,
        in_specs=[SMEM if a.dtype == jnp.int32 and a.ndim == 1 else VMEM for a in ins],
        out_specs=[VMEM] * len(outs),
        scratch_shapes=list(scratch),
        compiler_params=pltpu.CompilerParams(vmem_limit_bytes=32 << 20),
        cost_estimate=pl.CostEstimate(flops=flops, bytes_accessed=moved, transcendentals=0),
        name=name,
    )(*ins)


def shaped(shape, dtype):
    return jax.ShapeDtypeStruct(shape, dtype)


def dot(a, b, contract=((1,), (0,))):
    return lax.dot_general(a, b, (contract, ((), ())), preferred_element_type=F32)


def ring(axis, step, periodic):
    count = lax.axis_size(axis)
    pairs = [(i, i + step) for i in range(count) if 0 <= i + step < count]
    if periodic:
        pairs = [(i, (i + step) % count) for i in range(count)]
    return pairs


def swap_half(value):
    return lax.ppermute(value, "half", [(0, 1), (1, 0)])


def to_neighbours(low_phi, high_phi, low_eta, high_eta):
    from_high = lax.ppermute(low_phi, "phi", ring("phi", -1, True))
    from_low = lax.ppermute(high_phi, "phi", ring("phi", 1, True))
    if lax.axis_size("eta") == 2:
        return [from_low, from_high, lax.ppermute(low_eta, "eta", [(0, 1), (1, 0)])]
    from_upper = lax.ppermute(low_eta, "eta", ring("eta", -1, False))
    from_lower = lax.ppermute(high_eta, "eta", ring("eta", 1, False))
    return [from_low, from_high, from_lower, from_upper]


def build_kernel(own, pair, src, dst, info, tiles, weights, mask, m_out, mt_out, w_out, acc, acct):
    block = tiles.shape[1]
    slots = tiles.shape[0]
    acc[...] = jnp.zeros_like(acc)
    acct[...] = jnp.zeros_like(acct)
    half = info[0]
    eta = info[1]
    for t in range(slots):
        source = src[t]
        target = dst[t]
        column = jnp.where(source > own + 2, own + 2, source) if pair else source
        live = target >= 0
        if pair:
            outside = ((source == own + 2) & (eta == 0)) | ((source == own + 3) & (eta == 1))
            live = live & jnp.logical_not(outside)
        row = jnp.where(target >= half * own, target - half * own, target - half * own + 2 * own)

        @pl.when(live)
        def _():
            tile = tiles[t].astype(F32)
            rows = pl.ds(pl.multiple_of(row * block, block), block)
            columns = pl.ds(pl.multiple_of(column * block, block), block)
            acc[rows, columns] += tile
            acct[columns, rows] += tile.T

    m_out[...] = acc[...].astype(BF16)
    mt_out[...] = acct[...].astype(BF16)
    layers, width, grid = weights.shape[0], weights.shape[1], mask.shape[1]
    side = width // grid
    spread = (
        lax.broadcasted_iota(jnp.int32, (width, grid), 0) // side
        == lax.broadcasted_iota(jnp.int32, (width, grid), 1)
    ).astype(F32)
    for layer in range(layers):
        keep = mask[layer].astype(F32)
        full = dot(dot(spread, keep), spread, ((1,), (1,)))
        w_out[layer] = (weights[layer].astype(F32) * full).astype(BF16)


def gather_kernel(count, matrix, *refs):
    sources, (own_out, other_out) = refs[:count], refs[count:]
    rows = own_out.shape[0]
    stacked = jnp.concatenate([r[...] for r in sources], axis=0)
    total = dot(matrix[...], stacked)
    own_out[...] = total[:rows]
    other_out[...] = total[rows:].astype(BF16)


def live_rows(info, rows, width):
    first = info[0] * rows
    row = first + lax.broadcasted_iota(jnp.int32, (rows, width), 0)
    return (row < info[2]).astype(F32)


def forward_kernel(info, state, own, other, weight, x_out, edge_out, rest_out, slope_out):
    rows, width = x_out.shape
    block = edge_out.shape[0]
    hfloat = state[...].astype(F32)
    mixed = (hfloat + own[...].astype(BF16).astype(F32) + other[...].astype(F32)).astype(BF16)
    x_out[...] = mixed
    pre = dot(mixed, weight[...])
    live = live_rows(info, rows, width)
    sigma = jax.nn.sigmoid(pre)
    new = (live * (hfloat + pre * sigma)).astype(BF16)
    edge_out[...] = new[:block]
    rest_out[...] = new[block:]
    slope_out[...] = live * sigma * (1.0 + pre * (1.0 - sigma))


def last_kernel(
    info, edge, rest, own, other, weight, cot, x_out, final_out, dz_out, dzo_out, dx_out
):
    rows, width = x_out.shape
    hfloat = jnp.concatenate([edge[...], rest[...]], axis=0).astype(F32)
    mixed = (hfloat + own[...].astype(BF16).astype(F32) + other[...].astype(F32)).astype(BF16)
    x_out[...] = mixed
    pre = dot(mixed, weight[...])
    live = live_rows(info, rows, width)
    sigma = jax.nn.sigmoid(pre)
    final_out[...] = (live * (hfloat + pre * sigma)).astype(BF16)
    delta = cot[...].astype(F32) * live * sigma * (1.0 + pre * (1.0 - sigma))
    delta = delta.astype(BF16)
    split_columns(info, delta, dz_out, dzo_out)
    dx_out[...] = dot(delta, weight[...], ((1,), (1,))).astype(BF16)


def split_columns(info, delta, mine_out, theirs_out):
    middle = delta.shape[1] // 2
    first = info[0] == 0
    left, right = delta[:, :middle], delta[:, middle:]
    mine_out[...] = jnp.where(first, left, right)
    theirs_out[...] = jnp.where(first, right, left)


def spread_kernel(mt, dx, dx_other, *outs):
    block = outs[0].shape[0]
    whole = jnp.concatenate([dx[...], dx_other[...]], axis=0)
    start = mt.shape[0] - block * len(outs)
    total = dot(mt[start:, :], whole).astype(BF16)
    for i, out in enumerate(outs):
        out[...] = total[i * block : (i + 1) * block]


def own_kernel(info, mt, dx, dx_other, cot, up_out):
    rows, width = up_out.shape
    whole = jnp.concatenate([dx[...], dx_other[...]], axis=0)
    live = live_rows(info, rows, width)
    up_out[...] = live * cot[...].astype(F32) + dx[...].astype(F32) + dot(mt[:rows, :], whole)


def delta_kernel(info, up, slope, *refs):
    arrived, (dz_out, dzo_out) = refs[:-2], refs[-2:]
    block = arrived[0].shape[0]
    extra = arrived[0][...].astype(F32)
    for r in arrived[1:]:
        extra = extra + r[...].astype(F32)
    upstream = jnp.concatenate([up[:block, :] + extra, up[block:, :]], axis=0)
    delta = (upstream * slope[...]).astype(BF16)
    split_columns(info, delta, dz_out, dzo_out)


def grad_kernel(parts, info, x, x_other, dz, dz_other, own_out, *refs):
    sends, total = refs[:-1], refs[-1]
    total[...] = dot(x[...], dz[...], ((0,), (0,))) + dot(x_other[...], dz_other[...], ((0,), (0,)))
    span = own_out.shape[0]
    place = info[3]
    for step in range(parts):
        target = lax.rem(place + step, parts)
        part = total[pl.ds(pl.multiple_of(target * span, span), span), :]
        if step == 0:
            own_out[...] = part
        else:
            sends[step - 1][...] = part.astype(BF16)


def sum_kernel(own, *refs):
    total = own[...].astype(F32)
    for r in refs[:-1]:
        total = total + r[...].astype(F32)
    refs[-1][...] = total.astype(BF16)


def finish_kernel(info, *refs):
    ins, out = refs[:-1], refs[-1]
    layers, rows, width = out.shape
    mask_rows = ins[-1]
    middle = width // 2
    first = info[0] == 0
    for layer in range(layers):
        mine, theirs = ins[2 * layer][...].astype(F32), ins[2 * layer + 1][...].astype(F32)
        keep = mask_rows[layer]
        out[layer, :, :middle] = jnp.where(first, mine, theirs) * keep[:, :middle]
        out[layer, :, middle:] = jnp.where(first, theirs, mine) * keep[:, middle:]


def phi_share(info, x, x_other, dz, dz_other):
    parts = lax.axis_size("phi")
    width, columns = x.shape[1], dz.shape[1]
    span = width // parts
    flops = 4 * x.shape[0] * width * columns
    if parts > 8:
        whole = call(
            functools.partial(grad_kernel, 1),
            (info, x, x_other, dz, dz_other),
            [shaped((width, columns), F32)],
            [pltpu.VMEM((width, columns), F32)],
            flops,
            "grad_whole",
        )[0]
        return lax.psum_scatter(whole.astype(BF16), "phi", scatter_dimension=0, tiled=True)
    own, *sends = call(
        functools.partial(grad_kernel, parts),
        (info, x, x_other, dz, dz_other),
        [shaped((span, columns), F32)] + [shaped((span, columns), BF16)] * (parts - 1),
        [pltpu.VMEM((width, columns), F32)],
        flops,
        "grad",
    )
    arrived = [
        lax.ppermute(sends[step - 1], "phi", ring("phi", step, True)) for step in range(1, parts)
    ]
    return call(
        sum_kernel, (own, *arrived), [shaped((span, columns), BF16)], name="phi_sum"
    )[0]


def eta_sum(share):
    if lax.axis_size("eta") == 2:
        arrived = [lax.ppermute(share, "eta", [(0, 1), (1, 0)])]
        return call(sum_kernel, (share, *arrived), [shaped(share.shape, BF16)], name="eta_sum")[0]
    gathered = lax.all_gather(share, "eta", axis=0)
    return jnp.sum(gathered.astype(F32), axis=0).astype(BF16)


def body(feats, cotangent, tiles, tile_src, tile_dst, weights, mask, counts):
    rows, width = feats.shape[2], feats.shape[3]
    block = tiles.shape[3]
    own = rows // block
    pair = lax.axis_size("eta") == 2
    rims = 3 if pair else 4
    layers, grid = weights.shape[0], mask.shape[1]
    side = width // grid
    info = jnp.stack(
        [lax.axis_index("half"), lax.axis_index("eta"), counts[0, 0], lax.axis_index("phi")]
    ).astype(jnp.int32)
    state = feats[0, 0]
    cot = cotangent[0, 0]
    height, depth = 2 * rows, rows + rims * block

    edge = state[:block]
    arrived = to_neighbours(edge, edge, edge, edge)
    matrix, matrix_t, masked = call(
        functools.partial(build_kernel, own, pair),
        (tile_src[0, 0], tile_dst[0, 0], info, tiles[0, 0], weights, mask),
        [shaped((height, depth), BF16), shaped((depth, height), BF16), shaped(weights.shape, BF16)],
        [pltpu.VMEM((height, depth), F32), pltpu.VMEM((depth, height), F32)],
        10_000_000,
        "build",
    )
    agg_flops = 2 * height * depth * width
    dense_flops = 2 * rows * width * width

    own_part, other_part = call(
        functools.partial(gather_kernel, 1 + rims),
        (matrix, state, *arrived),
        [shaped((rows, width), F32), shaped((rows, width), BF16)],
        flops=agg_flops,
        name="gather0",
    )
    received = swap_half(other_part)
    x0, edge, rest, slope0 = call(
        forward_kernel,
        (info, state, own_part, received, masked[0]),
        [
            shaped((rows, width), BF16),
            shaped((block, width), BF16),
            shaped((rows - block, width), BF16),
            shaped((rows, width), F32),
        ],
        flops=dense_flops,
        name="forward0",
    )
    arrived = to_neighbours(edge, edge, edge, edge)
    x0_other = swap_half(x0)
    own_part, other_part = call(
        functools.partial(gather_kernel, 2 + rims),
        (matrix, edge, rest, *arrived),
        [shaped((rows, width), F32), shaped((rows, width), BF16)],
        flops=agg_flops,
        name="gather1",
    )
    received = swap_half(other_part)
    x1, final, dz1, dz1_send, dx = call(
        last_kernel,
        (info, edge, rest, own_part, received, masked[1], cot),
        [
            shaped((rows, width), BF16),
            shaped((rows, width), BF16),
            shaped((rows, width // 2), BF16),
            shaped((rows, width // 2), BF16),
            shaped((rows, width), BF16),
        ],
        flops=2 * dense_flops,
        name="last",
    )
    dx_other = swap_half(dx)
    dz1_other = swap_half(dz1_send)
    x1_other = swap_half(x1)
    back = call(
        spread_kernel,
        (matrix_t, dx, dx_other),
        [shaped((block, width), BF16)] * rims,
        flops=2 * rims * block * height * width,
        name="spread",
    )
    if pair:
        arrived = to_neighbours(back[0], back[1], back[2], back[2])
    else:
        arrived = to_neighbours(*back)
    upstream = call(
        own_kernel,
        (info, matrix_t, dx, dx_other, cot),
        [shaped((rows, width), F32)],
        flops=2 * rows * height * width,
        name="own",
    )[0]
    share1 = phi_share(info, x1, x1_other, dz1, dz1_other)
    dz0, dz0_send = call(
        delta_kernel,
        (info, upstream, slope0, *arrived),
        [shaped((rows, width // 2), BF16), shaped((rows, width // 2), BF16)],
        name="delta",
    )
    dz0_other = swap_half(dz0_send)
    share0 = phi_share(info, x0, x0_other, dz0, dz0_other)
    total1 = eta_sum(share1)
    total0 = eta_sum(share0)
    other1 = swap_half(total1)
    other0 = swap_half(total0)

    span = width // lax.axis_size("phi")
    row_ids = (lax.axis_index("phi") * span + jnp.arange(span, dtype=jnp.int32)) // side
    chosen = jnp.take(mask, row_ids, axis=1)
    keep = jnp.broadcast_to(chosen[..., None], (layers, span, grid, side)).reshape(
        layers, span, width
    )
    result = call(
        finish_kernel,
        (info, total0, other0, total1, other1, keep.astype(F32)),
        [shaped((layers, span, width), F32)],
        name="finish",
    )[0]
    return final[None, None], result


def solution(mesh):
    in_specs = (
        P(("group", "phi"), "eta", "half", None),
        P(("group", "phi"), "eta", "half", None),
        P(("group", "phi"), "eta", "half", None, None),
        P(("group", "phi"), "eta", "half"),
        P(("group", "phi"), "eta", "half"),
        P(),
        P(),
        P(("group", "phi"), "eta"),
    )
    out_specs = (P(("group", "phi"), "eta", "half", None), P("group", "phi", None))
    return jax.shard_map(body, mesh=mesh, in_specs=in_specs, out_specs=out_specs, check_vma=False)
```

```python
import functools

import jax
import jax.numpy as jnp
from jax import lax
from jax.experimental import pallas as pl
from jax.experimental.pallas import tpu as pltpu
from jax.sharding import PartitionSpec as P

BF16 = jnp.bfloat16
F32 = jnp.float32
VMEM = pl.BlockSpec(memory_space=pltpu.VMEM)
SMEM = pl.BlockSpec(memory_space=pltpu.SMEM)
ANY = pl.BlockSpec(memory_space=pl.ANY)
NOTE = 16


def call(kernel, ins, outs, scratch=(), flops=0, name=None, far=()):
    moved = sum(a.size * a.dtype.itemsize for a in ins)
    moved += sum(a.size * a.dtype.itemsize for a in outs)
    return pl.pallas_call(
        kernel,
        out_shape=outs,
        in_specs=[
            ANY if i in far else SMEM if a.dtype == jnp.int32 and a.ndim == 1 else VMEM
            for i, a in enumerate(ins)
        ],
        out_specs=[VMEM] * len(outs),
        scratch_shapes=list(scratch),
        compiler_params=pltpu.CompilerParams(vmem_limit_bytes=32 << 20),
        cost_estimate=pl.CostEstimate(flops=flops, bytes_accessed=moved, transcendentals=0),
        name=name,
    )(*ins)


def shaped(shape, dtype):
    return jax.ShapeDtypeStruct(shape, dtype)


def dot(a, b, contract=((1,), (0,))):
    return lax.dot_general(a, b, (contract, ((), ())), preferred_element_type=F32)


def ring(axis, step, periodic):
    count = lax.axis_size(axis)
    pairs = [(i, i + step) for i in range(count) if 0 <= i + step < count]
    if periodic:
        pairs = [(i, (i + step) % count) for i in range(count)]
    return pairs


def swap_half(value):
    return lax.ppermute(value, "half", [(0, 1), (1, 0)])


def to_neighbours(low_phi, high_phi, low_eta, high_eta):
    from_high = lax.ppermute(low_phi, "phi", ring("phi", -1, True))
    from_low = lax.ppermute(high_phi, "phi", ring("phi", 1, True))
    if lax.axis_size("eta") == 2:
        return [from_low, from_high, lax.ppermute(low_eta, "eta", [(0, 1), (1, 0)])]
    from_upper = lax.ppermute(low_eta, "eta", ring("eta", -1, False))
    from_lower = lax.ppermute(high_eta, "eta", ring("eta", 1, False))
    return [from_low, from_high, from_lower, from_upper]


def keep_full(mask, side):
    grid = mask.shape[0]
    width = grid * side
    spread = (
        lax.broadcasted_iota(jnp.int32, (width, grid), 0) // side
        == lax.broadcasted_iota(jnp.int32, (width, grid), 1)
    ).astype(F32)
    return dot(dot(spread, mask.astype(F32)), spread, ((1,), (1,)))


def build_kernel(own, pair, src, dst, info, tiles, weights, mask, m_out, w_out, tbuf, wbuf, kbuf, acc, sem):
    copies = [
        pltpu.make_async_copy(tiles, tbuf, sem.at[0]),
        pltpu.make_async_copy(mask, kbuf, sem.at[1]),
        pltpu.make_async_copy(weights.at[0], wbuf, sem.at[2]),
    ]
    for copy in copies:
        copy.start()
    slots, block = tbuf.shape[0], tbuf.shape[1]
    acc[...] = jnp.zeros_like(acc)
    half = info[0]
    eta = info[1]
    copies[0].wait()
    for t in range(slots):
        source = src[t]
        target = dst[t]
        column = jnp.where(source > own + 2, own + 2, source) if pair else source
        live = target >= 0
        if pair:
            outside = ((source == own + 2) & (eta == 0)) | ((source == own + 3) & (eta == 1))
            live = live & jnp.logical_not(outside)
        row = jnp.where(target >= half * own, target - half * own, target - half * own + 2 * own)

        @pl.when(live)
        def _():
            rows = pl.ds(pl.multiple_of(row * block, block), block)
            columns = pl.ds(pl.multiple_of(column * block, block), block)
            acc[rows, columns] += tbuf[t].astype(F32)

    m_out[...] = acc[...].astype(BF16)
    copies[1].wait()
    full = keep_full(kbuf[0], wbuf.shape[0] // kbuf.shape[1])
    copies[2].wait()
    w_out[...] = (wbuf[...].astype(F32) * full).astype(BF16)


def later_kernel(matrix, weights, mask, mt_out, w_out):
    mt_out[...] = matrix[...].T
    layers, width = weights.shape[0], weights.shape[1]
    for layer in range(1, layers):
        full = keep_full(mask[layer], width // mask.shape[1])
        w_out[layer - 1] = (weights[layer].astype(F32) * full).astype(BF16)


def gather_kernel(count, matrix, *refs):
    sources, (own_out, other_out) = refs[:count], refs[count:]
    rows, block = own_out.shape[0], refs[1].shape[0] - NOTE
    parts = [sources[0][...]] + [r[:block, :] for r in sources[1:]]
    total = dot(matrix[...], jnp.concatenate(parts, axis=0)).astype(BF16)
    own_out[...] = total[:rows]
    other_out[...] = total[rows:]


def mix(state, own, other):
    hfloat = state.astype(F32)
    return hfloat, (hfloat + own.astype(F32) + other.astype(F32)).astype(BF16)


def edge_kernel(state, own, other, out):
    block = out.shape[0]
    out[...] = mix(state[:block, :], own[:block, :], other[:block, :])[1]


def live_rows(info, rows, width):
    first = info[0] * rows
    row = first + lax.broadcasted_iota(jnp.int32, (rows, width), 0)
    return (row < info[2]).astype(F32)


def forward_kernel(info, state, own, other, weight, x_out, new_out, slope_out):
    rows, width = x_out.shape
    hfloat, mixed = mix(state[...], own[...], other[...])
    x_out[...] = mixed
    pre = dot(mixed, weight[...])
    live = live_rows(info, rows, width)
    sigma = jax.nn.sigmoid(pre)
    new_out[...] = (live * (hfloat + pre * sigma)).astype(BF16)
    slope_out[...] = live * sigma * (1.0 + pre * (1.0 - sigma))


def rim_kernel(count, matrix, weight, new, *refs):
    starts, mixes = refs[:count], refs[count : 2 * count]
    own_out, other_out, slope_out = refs[2 * count :]
    block, width = mixes[0].shape
    rows = own_out.shape[0]
    pre_all = dot(jnp.concatenate([r[...] for r in mixes], axis=0), weight[...])
    parts = [new[...]]
    for i in range(count):
        pre = pre_all[i * block : (i + 1) * block]
        note = starts[i][block : block + NOTE, :].astype(F32)[:1, :]
        row = lax.broadcasted_iota(jnp.int32, (block, width), 0).astype(F32)
        live = (row < note).astype(F32)
        sigma = jax.nn.sigmoid(pre)
        hfloat = starts[i][:block, :].astype(F32)
        parts.append((live * (hfloat + pre * sigma)).astype(BF16))
        slope_out[i * block : (i + 1) * block, :] = live * sigma * (1.0 + pre * (1.0 - sigma))
    total = dot(matrix[...], jnp.concatenate(parts, axis=0)).astype(BF16)
    own_out[...] = total[:rows]
    other_out[...] = total[rows:]


def last_kernel(info, state, own, other, weight, cot, x_out, final_out, dz_out, dx_out):
    rows, width = x_out.shape
    hfloat, mixed = mix(state[...], own[...], other[...])
    x_out[...] = mixed
    pre = dot(mixed, weight[...])
    live = live_rows(info, rows, width)
    sigma = jax.nn.sigmoid(pre)
    delta = cot[...].astype(F32) * live * sigma * (1.0 + pre * (1.0 - sigma))
    delta = delta.astype(BF16)
    dz_out[...] = delta
    dx_out[...] = dot(delta, weight[...], ((1,), (1,))).astype(BF16)
    final_out[...] = (live * (hfloat + pre * sigma)).astype(BF16)


def split_columns(info, value, mine_out, theirs_out):
    middle = value.shape[1] // 2
    first = info[0] == 0
    left, right = value[:, :middle], value[:, middle:]
    mine_out[...] = jnp.where(first, left, right)
    theirs_out[...] = jnp.where(first, right, left).astype(BF16)


def grad_kernel(info, x, dz, mine_out, theirs_out):
    split_columns(info, dot(x[...], dz[...], ((0,), (0,))), mine_out, theirs_out)


def back_kernel(count, info, mt, dx, dx_other, cot, slope, slope_rim, x, *refs):
    mixes, (mine_out, theirs_out) = refs[:count], refs[count:]
    rows = dx.shape[0]
    whole = jnp.concatenate([dx[...], dx_other[...]], axis=0)
    total = dot(mt[...], whole)
    upstream = cot[...].astype(F32) + dx[...].astype(F32) + total[:rows]
    delta = (upstream * slope[...]).astype(BF16)
    delta_rim = (total[rows:] * slope_rim[...]).astype(BF16)
    sources = jnp.concatenate([x[...]] + [r[...] for r in mixes], axis=0)
    deltas = jnp.concatenate([delta, delta_rim], axis=0)
    split_columns(info, dot(sources, deltas, ((0,), (0,))), mine_out, theirs_out)


def share_kernel(parts, layers, info, *refs):
    ins, outs = refs[: 2 * layers], refs[2 * layers :]
    span = outs[0].shape[0] // layers
    for step in range(parts):
        target = lax.rem(info[3] + step, parts)
        place = pl.ds(pl.multiple_of(target * span, span), span)
        for layer in range(layers):
            mine, arrived = ins[2 * layer], ins[2 * layer + 1]
            part = mine[place, :] + arrived[place, :].astype(F32)
            outs[step][layer * span : (layer + 1) * span, :] = part.astype(outs[step].dtype)


def sum_kernel(own, *refs):
    total = own[...].astype(F32)
    for r in refs[:-1]:
        total = total + r[...].astype(F32)
    refs[-1][...] = total.astype(BF16)


def finish_kernel(info, mine_ref, theirs_ref, keep, out):
    layers, rows, width = out.shape
    middle = width // 2
    first = info[0] == 0
    for layer in range(layers):
        part = slice(layer * rows, (layer + 1) * rows)
        mine, theirs = mine_ref[part, :].astype(F32), theirs_ref[part, :].astype(F32)
        kept = keep[layer]
        out[layer, :, :middle] = jnp.where(first, mine, theirs) * kept[:, :middle]
        out[layer, :, middle:] = jnp.where(first, theirs, mine) * kept[:, middle:]


def phi_share(info, pieces, layers):
    parts = lax.axis_size("phi")
    width, columns = pieces[0].shape
    span = width // parts
    if parts > 8:
        totals = [
            (pieces[2 * i] + pieces[2 * i + 1].astype(F32)).astype(BF16) for i in range(layers)
        ]
        shares = lax.psum_scatter(jnp.stack(totals), "phi", scatter_dimension=1, tiled=True)
        return shares.reshape(layers * span, columns)
    own, *sends = call(
        functools.partial(share_kernel, parts, layers),
        (info, *pieces),
        [shaped((layers * span, columns), F32)]
        + [shaped((layers * span, columns), BF16)] * (parts - 1),
        name="share",
    )
    arrived = [
        lax.ppermute(sends[step - 1], "phi", ring("phi", step, True)) for step in range(1, parts)
    ]
    return call(sum_kernel, (own, *arrived), [shaped(own.shape, BF16)], name="phi_sum")[0]


def eta_sum(share):
    if lax.axis_size("eta") == 2:
        arrived = lax.ppermute(share, "eta", [(0, 1), (1, 0)])
        return call(sum_kernel, (share, arrived), [shaped(share.shape, BF16)], name="eta_sum")[0]
    gathered = lax.all_gather(share, "eta", axis=0)
    return jnp.sum(gathered.astype(F32), axis=0).astype(BF16)


def body(feats, cotangent, tiles, tile_src, tile_dst, weights, mask, counts):
    rows, width = feats.shape[2], feats.shape[3]
    block = tiles.shape[3]
    own = rows // block
    pair = lax.axis_size("eta") == 2
    rims = 3 if pair else 4
    layers, grid = weights.shape[0], mask.shape[1]
    side = width // grid
    half_here = lax.axis_index("half")
    count = counts[0, 0]
    info = jnp.stack([half_here, lax.axis_index("eta"), count, lax.axis_index("phi")])
    info = info.astype(jnp.int32)
    state = feats[0, 0]
    cot = cotangent[0, 0]
    height, depth = 2 * rows, rows + rims * block

    note = jnp.clip(count - half_here * rows, 0, block).astype(BF16)
    edge = jnp.concatenate([state[:block], jnp.full((NOTE, width), note, BF16)], axis=0)
    starts = to_neighbours(edge, edge, edge, edge)
    matrix, masked0 = call(
        functools.partial(build_kernel, own, pair),
        (tile_src[0, 0], tile_dst[0, 0], info, tiles[0, 0], weights, mask),
        [shaped((height, depth), BF16), shaped((width, width), BF16)],
        [
            pltpu.VMEM(tiles.shape[2:], BF16),
            pltpu.VMEM((width, width), BF16),
            pltpu.VMEM(mask.shape, jnp.int32),
            pltpu.VMEM((height, depth), F32),
            pltpu.SemaphoreType.DMA((3,)),
        ],
        10_000_000,
        "build",
        (3, 4, 5),
    )
    agg_flops = 2 * height * depth * width
    dense_flops = 2 * rows * width * width
    wide = shaped((rows, width), BF16)

    own_part, other_part = call(
        functools.partial(gather_kernel, 1 + rims),
        (matrix, state, *starts),
        [wide, wide],
        flops=agg_flops,
        name="gather",
    )
    received = swap_half(other_part)
    edge = call(
        edge_kernel, (state, own_part, received), [shaped((block, width), BF16)], name="edge"
    )[0]
    mixes = to_neighbours(edge, edge, edge, edge)
    x0, new, slope0 = call(
        forward_kernel,
        (info, state, own_part, received, masked0),
        [wide, wide, shaped((rows, width), F32)],
        flops=dense_flops,
        name="forward",
    )
    matrix_t, masked = call(
        later_kernel,
        (matrix, weights, mask),
        [shaped((depth, height), BF16), shaped((layers - 1, width, width), BF16)],
        flops=10_000_000,
        name="later",
    )
    own_part, other_part, slope_rim = call(
        functools.partial(rim_kernel, rims),
        (matrix, masked0, new, *starts, *mixes),
        [wide, wide, shaped((rims * block, width), F32)],
        flops=agg_flops + 2 * dense_flops,
        name="rim",
    )
    received = swap_half(other_part)
    x1, final, dz1, dx = call(
        last_kernel,
        (info, new, own_part, received, masked[0], cot),
        [wide, wide, wide, wide],
        flops=2 * dense_flops,
        name="last",
    )
    dx_other = swap_half(dx)
    halves = [shaped((width, width // 2), F32), shaped((width, width // 2), BF16)]
    mine1, theirs1 = call(
        grad_kernel, (info, x1, dz1), halves, flops=dense_flops, name="grad"
    )
    arrived1 = swap_half(theirs1)
    mine0, theirs0 = call(
        functools.partial(back_kernel, rims),
        (info, matrix_t, dx, dx_other, cot, slope0, slope_rim, x0, *mixes),
        halves,
        flops=2 * agg_flops,
        name="back",
    )
    arrived0 = swap_half(theirs0)
    share = phi_share(info, (mine0, arrived0, mine1, arrived1), layers)
    total = eta_sum(share)
    theirs = swap_half(total)

    span = width // lax.axis_size("phi")
    row_ids = (lax.axis_index("phi") * span + jnp.arange(span, dtype=jnp.int32)) // side
    chosen = jnp.take(mask, row_ids, axis=1)
    keep = jnp.broadcast_to(chosen[..., None], (layers, span, grid, side)).reshape(
        layers, span, width
    )
    result = call(
        finish_kernel,
        (info, total, theirs, keep.astype(F32)),
        [shaped((layers, span, width), F32)],
        name="finish",
    )[0]
    return final[None, None], result


def solution(mesh):
    in_specs = (
        P(("group", "phi"), "eta", "half", None),
        P(("group", "phi"), "eta", "half", None),
        P(("group", "phi"), "eta", "half", None, None),
        P(("group", "phi"), "eta", "half"),
        P(("group", "phi"), "eta", "half"),
        P(),
        P(),
        P(("group", "phi"), "eta"),
    )
    out_specs = (P(("group", "phi"), "eta", "half", None), P("group", "phi", None))
    return jax.shard_map(body, mesh=mesh, in_specs=in_specs, out_specs=out_specs, check_vma=False)
```

```python
import functools

import jax
import jax.numpy as jnp
from jax import lax
from jax.experimental import pallas as pl
from jax.experimental.pallas import tpu as pltpu
from jax.sharding import PartitionSpec as P

BF16 = jnp.bfloat16
F32 = jnp.float32
VMEM = pl.BlockSpec(memory_space=pltpu.VMEM)
FAR = pl.BlockSpec(memory_space=pltpu.HBM)
DEAD = 2.0**100


def call(kernel, ins, outs, scratch=(), flops=0, name=None, far=False):
    moved = sum(a.size * a.dtype.itemsize for a in ins)
    moved += sum(a.size * a.dtype.itemsize for a in outs)
    if far:
        ins = [pltpu.with_memory_space_constraint(a, pltpu.HBM) for a in ins]
    return pl.pallas_call(
        kernel,
        out_shape=outs,
        in_specs=[FAR if far else VMEM] * len(ins),
        out_specs=[VMEM] * len(outs),
        scratch_shapes=list(scratch),
        compiler_params=pltpu.CompilerParams(vmem_limit_bytes=32 << 20),
        cost_estimate=pl.CostEstimate(flops=flops, bytes_accessed=moved, transcendentals=0),
        name=name,
    )(*ins)


def shaped(shape, dtype):
    return jax.ShapeDtypeStruct(shape, dtype)


def dot(a, b, contract=((1,), (0,))):
    return lax.dot_general(a, b, (contract, ((), ())), preferred_element_type=F32)


def ring(axis, step, periodic):
    count = lax.axis_size(axis)
    pairs = [(i, i + step) for i in range(count) if 0 <= i + step < count]
    if periodic:
        pairs = [(i, (i + step) % count) for i in range(count)]
    return pairs


def swap_half(value):
    return lax.ppermute(value, "half", [(0, 1), (1, 0)])


def to_neighbours(low_phi, high_phi, low_eta, high_eta):
    from_high = lax.ppermute(low_phi, "phi", ring("phi", -1, True))
    from_low = lax.ppermute(high_phi, "phi", ring("phi", 1, True))
    if lax.axis_size("eta") == 2:
        return [from_low, from_high, lax.ppermute(low_eta, "eta", [(0, 1), (1, 0)])]
    from_upper = lax.ppermute(low_eta, "eta", ring("eta", -1, False))
    from_lower = lax.ppermute(high_eta, "eta", ring("eta", 1, False))
    return [from_low, from_high, from_lower, from_upper]


def keep_full(mask, side):
    grid = mask.shape[0]
    width = grid * side
    spread = (
        lax.broadcasted_iota(jnp.int32, (width, grid), 0) // side
        == lax.broadcasted_iota(jnp.int32, (width, grid), 1)
    ).astype(F32)
    return dot(dot(spread, mask.astype(F32)), spread, ((1,), (1,)))


def build_kernel(own, pair, *refs):
    srcs, (m_out, w_out), bufs = refs[:5], refs[5:7], refs[7:12]
    acc, sem = refs[12:]
    src, dst, tbuf, kbuf, wbuf = bufs
    copies = [
        pltpu.make_async_copy(a.at[0] if i == 4 else a, b, sem.at[i])
        for i, (a, b) in enumerate(zip(srcs, bufs))
    ]
    for copy in copies:
        copy.start()
    slots, block = tbuf.shape[0], tbuf.shape[1]
    acc[...] = jnp.zeros_like(acc)
    half = lax.axis_index("half")
    eta = lax.axis_index("eta")
    for copy in copies[:3]:
        copy.wait()
    for t in range(slots):
        source = src[t]
        target = dst[t]
        column = jnp.where(source > own + 2, own + 2, source) if pair else source
        live = target >= 0
        if pair:
            outside = ((source == own + 2) & (eta == 0)) | ((source == own + 3) & (eta == 1))
            live = live & jnp.logical_not(outside)
        row = jnp.where(target >= half * own, target - half * own, target - half * own + 2 * own)

        @pl.when(live)
        def _():
            rows = pl.ds(pl.multiple_of(row * block, block), block)
            columns = pl.ds(pl.multiple_of(column * block, block), block)
            acc[rows, columns] += tbuf[t].astype(F32)

    m_out[...] = acc[...].astype(BF16)
    copies[3].wait()
    full = keep_full(kbuf[0], wbuf.shape[0] // kbuf.shape[1])
    copies[4].wait()
    w_out[...] = (wbuf[...].astype(F32) * full).astype(BF16)


def later_kernel(matrix, weights, mask, mt_out, w_out):
    mt_out[...] = matrix[...].T
    layers, width = weights.shape[0], weights.shape[1]
    for layer in range(1, layers):
        full = keep_full(mask[layer], width // mask.shape[1])
        w_out[layer - 1] = (weights[layer].astype(F32) * full).astype(BF16)


def gather_kernel(count, matrix, *refs):
    sources, (own_out, other_out) = refs[:count], refs[count:]
    rows = own_out.shape[0]
    stacked = jnp.concatenate([r[...] for r in sources], axis=0)
    total = dot(matrix[...], stacked).astype(BF16)
    own_out[...] = total[:rows]
    other_out[...] = total[rows:]


def mix(state, own, other):
    hfloat = state.astype(F32)
    return hfloat, (hfloat + own.astype(F32) + other.astype(F32)).astype(BF16)


def edge_kernel(count, state, own, other, out):
    block, width = out.shape
    mixed = mix(state[:block, :], own[:block, :], other[:block, :])[1].astype(F32)
    row = lax.broadcasted_iota(jnp.int32, (block, width), 0)
    out[...] = jnp.where(row < count[:1, :1], mixed, DEAD).astype(BF16)


def read_rim(ref):
    value = ref[...].astype(F32)
    live = value < 0.5 * DEAD
    return live.astype(F32), jnp.where(live, value, 0.0).astype(BF16)


def live_rows(count, rows, width):
    row = lax.broadcasted_iota(jnp.int32, (rows, width), 0)
    return (row < count[:1, :1]).astype(F32)


def forward_kernel(count, state, own, other, weight, x_out, new_out, slope_out):
    rows, width = x_out.shape
    hfloat, mixed = mix(state[...], own[...], other[...])
    x_out[...] = mixed
    pre = dot(mixed, weight[...])
    live = live_rows(count, rows, width)
    sigma = jax.nn.sigmoid(pre)
    new_out[...] = (live * (hfloat + pre * sigma)).astype(BF16)
    slope_out[...] = live * sigma * (1.0 + pre * (1.0 - sigma))


def rim_kernel(count, matrix, weight, new, *refs):
    starts, mixes = refs[:count], refs[count : 2 * count]
    own_out, other_out, slope_out = refs[2 * count :]
    block, width = mixes[0].shape
    rows = own_out.shape[0]
    rims = [read_rim(r) for r in mixes]
    pre_all = dot(jnp.concatenate([r[1] for r in rims], axis=0), weight[...])
    parts = [new[...]]
    for i in range(count):
        pre = pre_all[i * block : (i + 1) * block]
        live = rims[i][0]
        sigma = jax.nn.sigmoid(pre)
        hfloat = starts[i][...].astype(F32)
        parts.append((live * (hfloat + pre * sigma)).astype(BF16))
        slope_out[i * block : (i + 1) * block, :] = live * sigma * (1.0 + pre * (1.0 - sigma))
    total = dot(matrix[...], jnp.concatenate(parts, axis=0)).astype(BF16)
    own_out[...] = total[:rows]
    other_out[...] = total[rows:]


def last_kernel(count, state, own, other, weight, cot, x_out, final_out, dz_out, dx_out):
    rows, width = x_out.shape
    hfloat, mixed = mix(state[...], own[...], other[...])
    x_out[...] = mixed
    pre = dot(mixed, weight[...])
    live = live_rows(count, rows, width)
    sigma = jax.nn.sigmoid(pre)
    delta = cot[...].astype(F32) * live * sigma * (1.0 + pre * (1.0 - sigma))
    delta = delta.astype(BF16)
    dz_out[...] = delta
    dx_out[...] = dot(delta, weight[...], ((1,), (1,))).astype(BF16)
    final_out[...] = (live * (hfloat + pre * sigma)).astype(BF16)


def split_columns(value, mine_out, theirs_out):
    middle = value.shape[1] // 2
    first = lax.axis_index("half") == 0
    left, right = value[:, :middle], value[:, middle:]
    mine_out[...] = jnp.where(first, left, right)
    theirs_out[...] = jnp.where(first, right, left).astype(BF16)


def grad_kernel(x, dz, mine_out, theirs_out):
    split_columns(dot(x[...], dz[...], ((0,), (0,))), mine_out, theirs_out)


def turn_kernel(x, *refs):
    rims = [read_rim(r)[1] for r in refs[:-1]]
    refs[-1][...] = jnp.concatenate([x[...]] + rims, axis=0).T


def back_kernel(mt, dx, dx_other, cot, slope, slope_rim, xt, mine_out, theirs_out):
    rows = dx.shape[0]
    whole = jnp.concatenate([dx[...], dx_other[...]], axis=0)
    total = dot(mt[...], whole)
    upstream = cot[...].astype(F32) + dx[...].astype(F32) + total[:rows]
    delta = (upstream * slope[...]).astype(BF16)
    delta_rim = (total[rows:] * slope_rim[...]).astype(BF16)
    deltas = jnp.concatenate([delta, delta_rim], axis=0)
    split_columns(dot(xt[...], deltas), mine_out, theirs_out)


def fold_kernel(level, own, arrived, keep_out, send_out):
    parts = lax.axis_size("phi") >> level
    span = own.shape[0] // parts
    bit = lax.rem(lax.axis_index("phi") // (1 << level), 2)
    for pair in range(parts // 2):
        rows = slice(pair * span, (pair + 1) * span)
        for mine, out in ((bit, keep_out), (1 - bit, send_out)):
            place = pl.ds(pl.multiple_of((2 * pair + mine) * span, span), span)
            part = own[place, :] + arrived[place, :].astype(F32)
            out[rows, :] = part.astype(out.dtype)


def sum_kernel(own, *refs):
    total = own[...].astype(F32)
    for r in refs[:-1]:
        total = total + r[...].astype(F32)
    refs[-1][...] = total.astype(BF16)


def finish_kernel(*refs):
    keep, out = refs[-2:]
    layers, rows, width = out.shape
    middle = width // 2
    first = lax.axis_index("half") == 0
    for layer in range(layers):
        mine, theirs = refs[2 * layer][...].astype(F32), refs[2 * layer + 1][...].astype(F32)
        kept = keep[layer]
        out[layer, :, :middle] = jnp.where(first, mine, theirs) * kept[:, :middle]
        out[layer, :, middle:] = jnp.where(first, theirs, mine) * kept[:, middle:]


def phi_share(mine, theirs):
    arrived = swap_half(theirs)
    parts = lax.axis_size("phi")
    if parts & (parts - 1):
        total = (mine + arrived.astype(F32)).astype(BF16)
        return lax.psum_scatter(total, "phi", scatter_dimension=0, tiled=True)
    own = mine
    for level in range(parts.bit_length() - 1):
        shape = (own.shape[0] // 2, own.shape[1])
        own, send = call(
            functools.partial(fold_kernel, level),
            (own, arrived),
            [shaped(shape, F32), shaped(shape, BF16)],
            name="fold",
        )
        arrived = lax.ppermute(send, "phi", [(i, i ^ (1 << level)) for i in range(parts)])
    return call(sum_kernel, (own, arrived), [shaped(own.shape, BF16)], name="phi_sum")[0]


def eta_sum(share):
    if lax.axis_size("eta") == 2:
        arrived = lax.ppermute(share, "eta", [(0, 1), (1, 0)])
        return call(sum_kernel, (share, arrived), [shaped(share.shape, BF16)], name="eta_sum")[0]
    gathered = lax.all_gather(share, "eta", axis=0)
    return jnp.sum(gathered.astype(F32), axis=0).astype(BF16)


def body(feats, cotangent, tiles, tile_src, tile_dst, weights, mask, counts):
    rows, width = feats.shape[2], feats.shape[3]
    block = tiles.shape[3]
    own = rows // block
    pair = lax.axis_size("eta") == 2
    rims = 3 if pair else 4
    layers, grid = weights.shape[0], mask.shape[1]
    side = width // grid
    live_here = counts[0, 0] - lax.axis_index("half").astype(jnp.int32) * rows
    count = jnp.full((8, 128), live_here, jnp.int32)
    state = feats[0, 0]
    cot = cotangent[0, 0]
    height, depth = 2 * rows, rows + rims * block

    edge = state[:block]
    starts = to_neighbours(edge, edge, edge, edge)
    matrix, masked0 = call(
        functools.partial(build_kernel, own, pair),
        (tile_src[0, 0], tile_dst[0, 0], tiles[0, 0], mask, weights),
        [shaped((height, depth), BF16), shaped((width, width), BF16)],
        [
            pltpu.SMEM(tile_src.shape[2:], jnp.int32),
            pltpu.SMEM(tile_dst.shape[2:], jnp.int32),
            pltpu.VMEM(tiles.shape[2:], BF16),
            pltpu.VMEM(mask.shape, jnp.int32),
            pltpu.VMEM((width, width), BF16),
            pltpu.VMEM((height, depth), F32),
            pltpu.SemaphoreType.DMA((5,)),
        ],
        10_000_000,
        "build",
        True,
    )
    agg_flops = 2 * height * depth * width
    dense_flops = 2 * rows * width * width
    wide = shaped((rows, width), BF16)

    own_part, other_part = call(
        functools.partial(gather_kernel, 1 + rims),
        (matrix, state, *starts),
        [wide, wide],
        flops=agg_flops,
        name="gather",
    )
    received = swap_half(other_part)
    edge = call(
        edge_kernel, (count, state, own_part, received), [shaped((block, width), BF16)], name="edge"
    )[0]
    mixes = to_neighbours(edge, edge, edge, edge)
    x0, new, slope0 = call(
        forward_kernel,
        (count, state, own_part, received, masked0),
        [wide, wide, shaped((rows, width), F32)],
        flops=dense_flops,
        name="forward",
    )
    matrix_t, masked = call(
        later_kernel,
        (matrix, weights, mask),
        [shaped((depth, height), BF16), shaped((layers - 1, width, width), BF16)],
        flops=10_000_000,
        name="later",
    )
    own_part, other_part, slope_rim = call(
        functools.partial(rim_kernel, rims),
        (matrix, masked0, new, *starts, *mixes),
        [wide, wide, shaped((rims * block, width), F32)],
        flops=agg_flops + 2 * dense_flops,
        name="rim",
    )
    received = swap_half(other_part)
    x1, final, dz1, dx = call(
        last_kernel,
        (count, new, own_part, received, masked[0], cot),
        [wide, wide, wide, wide],
        flops=2 * dense_flops,
        name="last",
    )
    dx_other = swap_half(dx)
    halves = [shaped((width, width // 2), F32), shaped((width, width // 2), BF16)]
    mine1, theirs1 = call(
        grad_kernel, (x1, dz1), halves, flops=dense_flops, name="grad"
    )
    share1 = phi_share(mine1, theirs1)
    xt = call(
        turn_kernel, (x0, *mixes), [shaped((width, depth), BF16)], flops=1_000_000, name="turn"
    )[0]
    mine0, theirs0 = call(
        back_kernel,
        (matrix_t, dx, dx_other, cot, slope0, slope_rim, xt),
        halves,
        flops=2 * agg_flops,
        name="back",
    )
    share0 = phi_share(mine0, theirs0)
    total1 = eta_sum(share1)
    other1 = swap_half(total1)
    total0 = eta_sum(share0)
    other0 = swap_half(total0)

    span = width // lax.axis_size("phi")
    row_ids = (lax.axis_index("phi") * span + jnp.arange(span, dtype=jnp.int32)) // side
    chosen = jnp.take(mask, row_ids, axis=1)
    keep = jnp.broadcast_to(chosen[..., None], (layers, span, grid, side)).reshape(
        layers, span, width
    )
    result = call(
        finish_kernel,
        (total0, other0, total1, other1, keep.astype(F32)),
        [shaped((layers, span, width), F32)],
        name="finish",
    )[0]
    return final[None, None], result


def solution(mesh):
    in_specs = (
        P(("group", "phi"), "eta", "half", None),
        P(("group", "phi"), "eta", "half", None),
        P(("group", "phi"), "eta", "half", None, None),
        P(("group", "phi"), "eta", "half"),
        P(("group", "phi"), "eta", "half"),
        P(),
        P(),
        P(("group", "phi"), "eta"),
    )
    out_specs = (P(("group", "phi"), "eta", "half", None), P("group", "phi", None))
    return jax.shard_map(body, mesh=mesh, in_specs=in_specs, out_specs=out_specs, check_vma=False)
```

```python
import functools

import jax
import jax.numpy as jnp
from jax import lax
from jax.experimental import pallas as pl
from jax.experimental.pallas import tpu as pltpu
from jax.sharding import PartitionSpec as P

BF16 = jnp.bfloat16
F32 = jnp.float32
VMEM = pl.BlockSpec(memory_space=pltpu.VMEM)
FAR = pl.BlockSpec(memory_space=pltpu.HBM)
DEAD = 2.0**100


def call(kernel, ins, outs, scratch=(), flops=0, name=None, far=False):
    moved = sum(a.size * a.dtype.itemsize for a in ins)
    moved += sum(a.size * a.dtype.itemsize for a in outs)
    if far:
        ins = [pltpu.with_memory_space_constraint(a, pltpu.HBM) for a in ins]
    return pl.pallas_call(
        kernel,
        out_shape=outs,
        in_specs=[FAR if far else VMEM] * len(ins),
        out_specs=[VMEM] * len(outs),
        scratch_shapes=list(scratch),
        compiler_params=pltpu.CompilerParams(vmem_limit_bytes=32 << 20),
        cost_estimate=pl.CostEstimate(flops=flops, bytes_accessed=moved, transcendentals=0),
        name=name,
    )(*ins)


def shaped(shape, dtype):
    return jax.ShapeDtypeStruct(shape, dtype)


def dot(a, b, contract=((1,), (0,))):
    return lax.dot_general(a, b, (contract, ((), ())), preferred_element_type=F32)


def ring(axis, step, periodic):
    count = lax.axis_size(axis)
    pairs = [(i, i + step) for i in range(count) if 0 <= i + step < count]
    if periodic:
        pairs = [(i, (i + step) % count) for i in range(count)]
    return pairs


def swap_half(value):
    return lax.ppermute(value, "half", [(0, 1), (1, 0)])


def to_neighbours(low_phi, high_phi, low_eta, high_eta):
    from_high = lax.ppermute(low_phi, "phi", ring("phi", -1, True))
    from_low = lax.ppermute(high_phi, "phi", ring("phi", 1, True))
    if lax.axis_size("eta") == 2:
        return [from_low, from_high, lax.ppermute(low_eta, "eta", [(0, 1), (1, 0)])]
    from_upper = lax.ppermute(low_eta, "eta", ring("eta", -1, False))
    from_lower = lax.ppermute(high_eta, "eta", ring("eta", 1, False))
    return [from_low, from_high, from_lower, from_upper]


def keep_full(mask, side):
    grid = mask.shape[0]
    width = grid * side
    spread = (
        lax.broadcasted_iota(jnp.int32, (width, grid), 0) // side
        == lax.broadcasted_iota(jnp.int32, (width, grid), 1)
    ).astype(F32)
    return dot(dot(spread, mask.astype(F32)), spread, ((1,), (1,)))


def build_kernel(own, pair, *refs):
    srcs, (m_out, w_out), bufs = refs[:5], refs[5:7], refs[7:12]
    acc, sem = refs[12:]
    src, dst, tbuf, kbuf, wbuf = bufs
    copies = [
        pltpu.make_async_copy(a.at[0] if i == 4 else a, b, sem.at[i])
        for i, (a, b) in enumerate(zip(srcs, bufs))
    ]
    for copy in copies:
        copy.start()
    slots, block = tbuf.shape[0], tbuf.shape[1]
    acc[...] = jnp.zeros_like(acc)
    half = lax.axis_index("half")
    eta = lax.axis_index("eta")
    for copy in copies[:3]:
        copy.wait()
    for t in range(slots):
        source = src[t]
        target = dst[t]
        column = jnp.where(source > own + 2, own + 2, source) if pair else source
        live = target >= 0
        if pair:
            outside = ((source == own + 2) & (eta == 0)) | ((source == own + 3) & (eta == 1))
            live = live & jnp.logical_not(outside)
        row = jnp.where(target >= half * own, target - half * own, target - half * own + 2 * own)

        @pl.when(live)
        def _():
            rows = pl.ds(pl.multiple_of(row * block, block), block)
            columns = pl.ds(pl.multiple_of(column * block, block), block)
            acc[rows, columns] += tbuf[t].astype(F32)

    m_out[...] = acc[...].astype(BF16)
    copies[3].wait()
    full = keep_full(kbuf[0], wbuf.shape[0] // kbuf.shape[1])
    copies[4].wait()
    w_out[...] = (wbuf[...].astype(F32) * full).astype(BF16)


def later_kernel(matrix, weights, mask, mt_out, w_out):
    mt_out[...] = matrix[...].T
    layers, width = weights.shape[0], weights.shape[1]
    for layer in range(1, layers):
        full = keep_full(mask[layer], width // mask.shape[1])
        w_out[layer - 1] = (weights[layer].astype(F32) * full).astype(BF16)


def gather_kernel(count, matrix, *refs):
    sources, (own_out, other_out) = refs[:count], refs[count:]
    rows = own_out.shape[0]
    stacked = jnp.concatenate([r[...] for r in sources], axis=0)
    total = dot(matrix[...], stacked).astype(BF16)
    own_out[...] = total[:rows]
    other_out[...] = total[rows:]


def mix(state, own, other):
    hfloat = state.astype(F32)
    return hfloat, (hfloat + own.astype(F32) + other.astype(F32)).astype(BF16)


def edge_kernel(count, state, own, other, out):
    block, width = out.shape
    mixed = mix(state[:block, :], own[:block, :], other[:block, :])[1].astype(F32)
    row = lax.broadcasted_iota(jnp.int32, (block, width), 0)
    out[...] = jnp.where(row < count[:1, :1], mixed, DEAD).astype(BF16)


def read_rim(ref):
    value = ref[...].astype(F32)
    live = value < 0.5 * DEAD
    return live.astype(F32), jnp.where(live, value, 0.0).astype(BF16)


def live_rows(count, rows, width):
    row = lax.broadcasted_iota(jnp.int32, (rows, width), 0)
    return (row < count[:1, :1]).astype(F32)


def forward_kernel(count, state, own, other, weight, x_out, new_out, slope_out):
    rows, width = x_out.shape
    hfloat, mixed = mix(state[...], own[...], other[...])
    x_out[...] = mixed
    pre = dot(mixed, weight[...])
    live = live_rows(count, rows, width)
    sigma = jax.nn.sigmoid(pre)
    new_out[...] = (live * (hfloat + pre * sigma)).astype(BF16)
    slope_out[...] = live * sigma * (1.0 + pre * (1.0 - sigma))


def rim_kernel(count, matrix, weight, new, *refs):
    starts, mixes = refs[:count], refs[count : 2 * count]
    own_out, other_out, slope_out = refs[2 * count :]
    block, width = mixes[0].shape
    rows = own_out.shape[0]
    rims = [read_rim(r) for r in mixes]
    pre_all = dot(jnp.concatenate([r[1] for r in rims], axis=0), weight[...])
    parts = [new[...]]
    for i in range(count):
        pre = pre_all[i * block : (i + 1) * block]
        live = rims[i][0]
        sigma = jax.nn.sigmoid(pre)
        hfloat = starts[i][...].astype(F32)
        parts.append((live * (hfloat + pre * sigma)).astype(BF16))
        slope_out[i * block : (i + 1) * block, :] = live * sigma * (1.0 + pre * (1.0 - sigma))
    total = dot(matrix[...], jnp.concatenate(parts, axis=0)).astype(BF16)
    own_out[...] = total[:rows]
    other_out[...] = total[rows:]


def last_kernel(count, state, own, other, weight, cot, x_out, final_out, dz_out, dx_out):
    rows, width = x_out.shape
    hfloat, mixed = mix(state[...], own[...], other[...])
    x_out[...] = mixed
    pre = dot(mixed, weight[...])
    live = live_rows(count, rows, width)
    sigma = jax.nn.sigmoid(pre)
    delta = cot[...].astype(F32) * live * sigma * (1.0 + pre * (1.0 - sigma))
    delta = delta.astype(BF16)
    dz_out[...] = delta
    dx_out[...] = dot(delta, weight[...], ((1,), (1,))).astype(BF16)
    final_out[...] = (live * (hfloat + pre * sigma)).astype(BF16)


def emit_kernel(value, out):
    out[...] = value[...]


def split_columns(value, mine_out, theirs_out):
    middle = value.shape[1] // 2
    first = lax.axis_index("half") == 0
    left, right = value[:, :middle], value[:, middle:]
    mine_out[...] = jnp.where(first, left, right)
    theirs_out[...] = jnp.where(first, right, left).astype(BF16)


def grad_kernel(x, dz, mine_out, theirs_out):
    split_columns(dot(x[...], dz[...], ((0,), (0,))), mine_out, theirs_out)


def turn_kernel(x, *refs):
    rims = [read_rim(r)[1] for r in refs[:-1]]
    refs[-1][...] = jnp.concatenate([x[...]] + rims, axis=0).T


def back_kernel(mt, dx, dx_other, cot, slope, slope_rim, xt, mine_out, theirs_out):
    rows = dx.shape[0]
    whole = jnp.concatenate([dx[...], dx_other[...]], axis=0)
    total = dot(mt[...], whole)
    upstream = cot[...].astype(F32) + dx[...].astype(F32) + total[:rows]
    delta = (upstream * slope[...]).astype(BF16)
    delta_rim = (total[rows:] * slope_rim[...]).astype(BF16)
    deltas = jnp.concatenate([delta, delta_rim], axis=0)
    split_columns(dot(xt[...], deltas), mine_out, theirs_out)


def fold_kernel(level, own, arrived, keep_out, send_out):
    parts = lax.axis_size("phi") >> level
    span = own.shape[0] // parts
    bit = lax.rem(lax.axis_index("phi") // (1 << level), 2)
    for pair in range(parts // 2):
        rows = slice(pair * span, (pair + 1) * span)
        for mine, out in ((bit, keep_out), (1 - bit, send_out)):
            place = pl.ds(pl.multiple_of((2 * pair + mine) * span, span), span)
            part = own[place, :] + arrived[place, :].astype(F32)
            out[rows, :] = part.astype(out.dtype)


def sum_kernel(own, *refs):
    total = own[...].astype(F32)
    for r in refs[:-1]:
        total = total + r[...].astype(F32)
    refs[-1][...] = total.astype(BF16)


def finish_kernel(*refs):
    keep, out = refs[-2:]
    layers, rows, width = out.shape
    middle = width // 2
    first = lax.axis_index("half") == 0
    for layer in range(layers):
        mine, theirs = refs[2 * layer][...].astype(F32), refs[2 * layer + 1][...].astype(F32)
        kept = keep[layer]
        out[layer, :, :middle] = jnp.where(first, mine, theirs) * kept[:, :middle]
        out[layer, :, middle:] = jnp.where(first, theirs, mine) * kept[:, middle:]


def phi_share(mine, theirs):
    arrived = swap_half(theirs)
    parts = lax.axis_size("phi")
    if parts & (parts - 1):
        total = (mine + arrived.astype(F32)).astype(BF16)
        return lax.psum_scatter(total, "phi", scatter_dimension=0, tiled=True)
    own = mine
    for level in range(parts.bit_length() - 1):
        shape = (own.shape[0] // 2, own.shape[1])
        own, send = call(
            functools.partial(fold_kernel, level),
            (own, arrived),
            [shaped(shape, F32), shaped(shape, BF16)],
            name="fold",
        )
        arrived = lax.ppermute(send, "phi", [(i, i ^ (1 << level)) for i in range(parts)])
    return call(sum_kernel, (own, arrived), [shaped(own.shape, BF16)], name="phi_sum")[0]


def eta_sum(share):
    if lax.axis_size("eta") == 2:
        arrived = lax.ppermute(share, "eta", [(0, 1), (1, 0)])
        return call(sum_kernel, (share, arrived), [shaped(share.shape, BF16)], name="eta_sum")[0]
    gathered = lax.all_gather(share, "eta", axis=0)
    return jnp.sum(gathered.astype(F32), axis=0).astype(BF16)


def body(feats, cotangent, tiles, tile_src, tile_dst, weights, mask, counts):
    rows, width = feats.shape[2], feats.shape[3]
    block = tiles.shape[3]
    own = rows // block
    pair = lax.axis_size("eta") == 2
    rims = 3 if pair else 4
    layers, grid = weights.shape[0], mask.shape[1]
    side = width // grid
    live_here = counts[0, 0] - lax.axis_index("half").astype(jnp.int32) * rows
    count = jnp.full((8, 128), live_here, jnp.int32)
    state = feats[0, 0]
    cot = cotangent[0, 0]
    height, depth = 2 * rows, rows + rims * block

    edge = state[:block]
    starts = to_neighbours(edge, edge, edge, edge)
    matrix, masked0 = call(
        functools.partial(build_kernel, own, pair),
        (tile_src[0, 0], tile_dst[0, 0], tiles[0, 0], mask, weights),
        [shaped((height, depth), BF16), shaped((width, width), BF16)],
        [
            pltpu.SMEM(tile_src.shape[2:], jnp.int32),
            pltpu.SMEM(tile_dst.shape[2:], jnp.int32),
            pltpu.VMEM(tiles.shape[2:], BF16),
            pltpu.VMEM(mask.shape, jnp.int32),
            pltpu.VMEM((width, width), BF16),
            pltpu.VMEM((height, depth), F32),
            pltpu.SemaphoreType.DMA((5,)),
        ],
        10_000_000,
        "build",
        True,
    )
    agg_flops = 2 * height * depth * width
    dense_flops = 2 * rows * width * width
    wide = shaped((rows, width), BF16)

    own_part, other_part = call(
        functools.partial(gather_kernel, 1 + rims),
        (matrix, state, *starts),
        [wide, wide],
        flops=agg_flops,
        name="gather",
    )
    received = swap_half(other_part)
    edge = call(
        edge_kernel, (count, state, own_part, received), [shaped((block, width), BF16)], name="edge"
    )[0]
    mixes = to_neighbours(edge, edge, edge, edge)
    x0, new, slope0 = call(
        forward_kernel,
        (count, state, own_part, received, masked0),
        [wide, wide, shaped((rows, width), F32)],
        flops=dense_flops,
        name="forward",
    )
    matrix_t, masked = call(
        later_kernel,
        (matrix, weights, mask),
        [shaped((depth, height), BF16), shaped((layers - 1, width, width), BF16)],
        flops=10_000_000,
        name="later",
    )
    own_part, other_part, slope_rim = call(
        functools.partial(rim_kernel, rims),
        (matrix, masked0, new, *starts, *mixes),
        [wide, wide, shaped((rims * block, width), F32)],
        flops=agg_flops + 2 * dense_flops,
        name="rim",
    )
    received = swap_half(other_part)
    x1, final, dz1, dx = call(
        last_kernel,
        (count, new, own_part, received, masked[0], cot),
        [wide, wide, wide, wide],
        flops=2 * dense_flops,
        name="last",
    )
    dx_other = swap_half(dx)
    final = call(emit_kernel, (final,), [wide], name="emit")[0]
    halves = [shaped((width, width // 2), F32), shaped((width, width // 2), BF16)]
    mine1, theirs1 = call(
        grad_kernel, (x1, dz1), halves, flops=dense_flops, name="grad"
    )
    share1 = phi_share(mine1, theirs1)
    xt = call(
        turn_kernel, (x0, *mixes), [shaped((width, depth), BF16)], flops=1_000_000, name="turn"
    )[0]
    mine0, theirs0 = call(
        back_kernel,
        (matrix_t, dx, dx_other, cot, slope0, slope_rim, xt),
        halves,
        flops=2 * agg_flops,
        name="back",
    )
    share0 = phi_share(mine0, theirs0)
    total1 = eta_sum(share1)
    other1 = swap_half(total1)
    total0 = eta_sum(share0)
    other0 = swap_half(total0)

    span = width // lax.axis_size("phi")
    row_ids = (lax.axis_index("phi") * span + jnp.arange(span, dtype=jnp.int32)) // side
    chosen = jnp.take(mask, row_ids, axis=1)
    keep = jnp.broadcast_to(chosen[..., None], (layers, span, grid, side)).reshape(
        layers, span, width
    )
    result = call(
        finish_kernel,
        (total0, other0, total1, other1, keep.astype(F32)),
        [shaped((layers, span, width), F32)],
        name="finish",
    )[0]
    return final[None, None], result


def solution(mesh):
    in_specs = (
        P(("group", "phi"), "eta", "half", None),
        P(("group", "phi"), "eta", "half", None),
        P(("group", "phi"), "eta", "half", None, None),
        P(("group", "phi"), "eta", "half"),
        P(("group", "phi"), "eta", "half"),
        P(),
        P(),
        P(("group", "phi"), "eta"),
    )
    out_specs = (P(("group", "phi"), "eta", "half", None), P("group", "phi", None))
    return jax.shard_map(body, mesh=mesh, in_specs=in_specs, out_specs=out_specs, check_vma=False)
```

```python
import functools

import jax
import jax.numpy as jnp
from jax import lax
from jax.experimental import pallas as pl
from jax.experimental.pallas import tpu as pltpu
from jax.sharding import PartitionSpec as P

BF16 = jnp.bfloat16
F32 = jnp.float32
VMEM = pl.BlockSpec(memory_space=pltpu.VMEM)
FAR = pl.BlockSpec(memory_space=pltpu.HBM)
DEAD = 2.0**100


def call(kernel, ins, outs, scratch=(), flops=0, name=None, far=False):
    moved = sum(a.size * a.dtype.itemsize for a in ins)
    moved += sum(a.size * a.dtype.itemsize for a in outs)
    if far:
        ins = [pltpu.with_memory_space_constraint(a, pltpu.HBM) for a in ins]
    return pl.pallas_call(
        kernel,
        out_shape=outs,
        in_specs=[FAR if far else VMEM] * len(ins),
        out_specs=[VMEM] * len(outs),
        scratch_shapes=list(scratch),
        compiler_params=pltpu.CompilerParams(vmem_limit_bytes=32 << 20),
        cost_estimate=pl.CostEstimate(flops=flops, bytes_accessed=moved, transcendentals=0),
        name=name,
    )(*ins)


def shaped(shape, dtype):
    return jax.ShapeDtypeStruct(shape, dtype)


def dot(a, b, contract=((1,), (0,))):
    return lax.dot_general(a, b, (contract, ((), ())), preferred_element_type=F32)


def ring(axis, step, periodic):
    count = lax.axis_size(axis)
    pairs = [(i, i + step) for i in range(count) if 0 <= i + step < count]
    if periodic:
        pairs = [(i, (i + step) % count) for i in range(count)]
    return pairs


def swap_half(value):
    return lax.ppermute(value, "half", [(0, 1), (1, 0)])


def to_neighbours(low_phi, high_phi, low_eta, high_eta):
    from_high = lax.ppermute(low_phi, "phi", ring("phi", -1, True))
    from_low = lax.ppermute(high_phi, "phi", ring("phi", 1, True))
    if lax.axis_size("eta") == 2:
        return [from_low, from_high, lax.ppermute(low_eta, "eta", [(0, 1), (1, 0)])]
    from_upper = lax.ppermute(low_eta, "eta", ring("eta", -1, False))
    from_lower = lax.ppermute(high_eta, "eta", ring("eta", 1, False))
    return [from_low, from_high, from_lower, from_upper]


def keep_full(mask, side):
    grid = mask.shape[0]
    width = grid * side
    spread = (
        lax.broadcasted_iota(jnp.int32, (width, grid), 0) // side
        == lax.broadcasted_iota(jnp.int32, (width, grid), 1)
    ).astype(F32)
    return dot(dot(spread, mask.astype(F32)), spread, ((1,), (1,)))


def build_kernel(own, pair, *refs):
    srcs, (m_out, w_out), bufs = refs[:5], refs[5:7], refs[7:12]
    acc, sem = refs[12:]
    src, dst, tbuf, kbuf, wbuf = bufs
    copies = [
        pltpu.make_async_copy(a.at[0] if i == 4 else a, b, sem.at[i])
        for i, (a, b) in enumerate(zip(srcs, bufs))
    ]
    for copy in copies:
        copy.start()
    slots, block = tbuf.shape[0], tbuf.shape[1]
    acc[...] = jnp.zeros_like(acc)
    half = lax.axis_index("half")
    eta = lax.axis_index("eta")
    for copy in copies[:3]:
        copy.wait()
    for t in range(slots):
        source = src[t]
        target = dst[t]
        column = jnp.where(source > own + 2, own + 2, source) if pair else source
        live = target >= 0
        if pair:
            outside = ((source == own + 2) & (eta == 0)) | ((source == own + 3) & (eta == 1))
            live = live & jnp.logical_not(outside)
        row = jnp.where(target >= half * own, target - half * own, target - half * own + 2 * own)

        @pl.when(live)
        def _():
            rows = pl.ds(pl.multiple_of(row * block, block), block)
            columns = pl.ds(pl.multiple_of(column * block, block), block)
            acc[rows, columns] += tbuf[t].astype(F32)

    m_out[...] = acc[...].astype(BF16)
    copies[3].wait()
    full = keep_full(kbuf[0], wbuf.shape[0] // kbuf.shape[1])
    copies[4].wait()
    w_out[...] = (wbuf[...].astype(F32) * full).astype(BF16)


def later_kernel(matrix, weights, mask, mt_out, w_out):
    mt_out[...] = matrix[...].T
    layers, width = weights.shape[0], weights.shape[1]
    for layer in range(1, layers):
        full = keep_full(mask[layer], width // mask.shape[1])
        w_out[layer - 1] = (weights[layer].astype(F32) * full).astype(BF16)


def gather_kernel(count, matrix, *refs):
    sources, (own_out, other_out) = refs[:count], refs[count:]
    rows = own_out.shape[0]
    stacked = jnp.concatenate([r[...] for r in sources], axis=0)
    total = dot(matrix[...], stacked).astype(BF16)
    own_out[...] = total[:rows]
    other_out[...] = total[rows:]


def mix(state, own, other):
    hfloat = state.astype(F32)
    return hfloat, (hfloat + own.astype(F32) + other.astype(F32)).astype(BF16)


def edge_kernel(count, state, own, other, out):
    block, width = out.shape
    mixed = mix(state[:block, :], own[:block, :], other[:block, :])[1].astype(F32)
    row = lax.broadcasted_iota(jnp.int32, (block, width), 0)
    out[...] = jnp.where(row < count[:1, :1], mixed, DEAD).astype(BF16)


def read_rim(ref):
    value = ref[...].astype(F32)
    live = value < 0.5 * DEAD
    return live.astype(F32), jnp.where(live, value, 0.0).astype(BF16)


def live_rows(count, rows, width):
    row = lax.broadcasted_iota(jnp.int32, (rows, width), 0)
    return (row < count[:1, :1]).astype(F32)


def forward_kernel(count, state, own, other, weight, x_out, new_out, slope_out):
    rows, width = x_out.shape
    hfloat, mixed = mix(state[...], own[...], other[...])
    x_out[...] = mixed
    pre = dot(mixed, weight[...])
    live = live_rows(count, rows, width)
    sigma = jax.nn.sigmoid(pre)
    new_out[...] = (live * (hfloat + pre * sigma)).astype(BF16)
    slope_out[...] = live * sigma * (1.0 + pre * (1.0 - sigma))


def rim_kernel(count, matrix, weight, new, *refs):
    starts, mixes = refs[:count], refs[count : 2 * count]
    own_out, other_out, slope_out = refs[2 * count :]
    block, width = mixes[0].shape
    rows = own_out.shape[0]
    rims = [read_rim(r) for r in mixes]
    pre_all = dot(jnp.concatenate([r[1] for r in rims], axis=0), weight[...])
    parts = [new[...]]
    for i in range(count):
        pre = pre_all[i * block : (i + 1) * block]
        live = rims[i][0]
        sigma = jax.nn.sigmoid(pre)
        hfloat = starts[i][...].astype(F32)
        parts.append((live * (hfloat + pre * sigma)).astype(BF16))
        slope_out[i * block : (i + 1) * block, :] = live * sigma * (1.0 + pre * (1.0 - sigma))
    total = dot(matrix[...], jnp.concatenate(parts, axis=0)).astype(BF16)
    own_out[...] = total[:rows]
    other_out[...] = total[rows:]


def last_kernel(count, state, own, other, weight, cot, x_out, final_out, dz_out, dx_out):
    rows, width = x_out.shape
    hfloat, mixed = mix(state[...], own[...], other[...])
    x_out[...] = mixed
    pre = dot(mixed, weight[...])
    live = live_rows(count, rows, width)
    sigma = jax.nn.sigmoid(pre)
    delta = cot[...].astype(F32) * live * sigma * (1.0 + pre * (1.0 - sigma))
    delta = delta.astype(BF16)
    dz_out[...] = delta
    dx_out[...] = dot(delta, weight[...], ((1,), (1,))).astype(BF16)
    final_out[...] = (live * (hfloat + pre * sigma)).astype(BF16)


def emit_kernel(value, out):
    out[...] = value[...]


def split_columns(value, mine_out, theirs_out):
    middle = value.shape[1] // 2
    first = lax.axis_index("half") == 0
    left, right = value[:, :middle], value[:, middle:]
    mine_out[...] = jnp.where(first, left, right)
    theirs_out[...] = jnp.where(first, right, left).astype(BF16)


def grad_kernel(x, dz, mine_out, theirs_out):
    split_columns(dot(x[...], dz[...], ((0,), (0,))), mine_out, theirs_out)


def turn_kernel(after, x, *refs):
    rims = [read_rim(r)[1] for r in refs[:-1]]
    refs[-1][...] = jnp.concatenate([x[...]] + rims, axis=0).T


def back_kernel(mt, dx, dx_other, cot, slope, slope_rim, xt, mine_out, theirs_out):
    rows = dx.shape[0]
    whole = jnp.concatenate([dx[...], dx_other[...]], axis=0)
    total = dot(mt[...], whole)
    upstream = cot[...].astype(F32) + dx[...].astype(F32) + total[:rows]
    delta = (upstream * slope[...]).astype(BF16)
    delta_rim = (total[rows:] * slope_rim[...]).astype(BF16)
    deltas = jnp.concatenate([delta, delta_rim], axis=0)
    split_columns(dot(xt[...], deltas), mine_out, theirs_out)


def fold_kernel(level, own, arrived, keep_out, send_out):
    parts = lax.axis_size("phi") >> level
    span = own.shape[0] // parts
    bit = lax.rem(lax.axis_index("phi") // (1 << level), 2)
    for pair in range(parts // 2):
        rows = slice(pair * span, (pair + 1) * span)
        for mine, out in ((bit, keep_out), (1 - bit, send_out)):
            place = pl.ds(pl.multiple_of((2 * pair + mine) * span, span), span)
            part = own[place, :] + arrived[place, :].astype(F32)
            out[rows, :] = part.astype(out.dtype)


def sum_kernel(own, *refs):
    total = own[...].astype(F32)
    for r in refs[:-1]:
        total = total + r[...].astype(F32)
    refs[-1][...] = total.astype(BF16)


def finish_kernel(*refs):
    keep, out = refs[-2:]
    layers, rows, width = out.shape
    middle = width // 2
    first = lax.axis_index("half") == 0
    for layer in range(layers):
        mine, theirs = refs[2 * layer][...].astype(F32), refs[2 * layer + 1][...].astype(F32)
        kept = keep[layer]
        out[layer, :, :middle] = jnp.where(first, mine, theirs) * kept[:, :middle]
        out[layer, :, middle:] = jnp.where(first, theirs, mine) * kept[:, middle:]


def phi_share(mine, theirs):
    arrived = swap_half(theirs)
    parts = lax.axis_size("phi")
    if parts & (parts - 1):
        total = (mine + arrived.astype(F32)).astype(BF16)
        return lax.psum_scatter(total, "phi", scatter_dimension=0, tiled=True)
    own = mine
    for level in range(parts.bit_length() - 1):
        shape = (own.shape[0] // 2, own.shape[1])
        own, send = call(
            functools.partial(fold_kernel, level),
            (own, arrived),
            [shaped(shape, F32), shaped(shape, BF16)],
            name="fold",
        )
        arrived = lax.ppermute(send, "phi", [(i, i ^ (1 << level)) for i in range(parts)])
    return call(sum_kernel, (own, arrived), [shaped(own.shape, BF16)], name="phi_sum")[0]


def eta_sum(share):
    if lax.axis_size("eta") == 2:
        arrived = lax.ppermute(share, "eta", [(0, 1), (1, 0)])
        return call(sum_kernel, (share, arrived), [shaped(share.shape, BF16)], name="eta_sum")[0]
    gathered = lax.all_gather(share, "eta", axis=0)
    return jnp.sum(gathered.astype(F32), axis=0).astype(BF16)


def body(feats, cotangent, tiles, tile_src, tile_dst, weights, mask, counts):
    rows, width = feats.shape[2], feats.shape[3]
    block = tiles.shape[3]
    own = rows // block
    pair = lax.axis_size("eta") == 2
    rims = 3 if pair else 4
    layers, grid = weights.shape[0], mask.shape[1]
    side = width // grid
    live_here = counts[0, 0] - lax.axis_index("half").astype(jnp.int32) * rows
    count = jnp.full((8, 128), live_here, jnp.int32)
    state = feats[0, 0]
    cot = cotangent[0, 0]
    height, depth = 2 * rows, rows + rims * block

    edge = state[:block]
    starts = to_neighbours(edge, edge, edge, edge)
    matrix, masked0 = call(
        functools.partial(build_kernel, own, pair),
        (tile_src[0, 0], tile_dst[0, 0], tiles[0, 0], mask, weights),
        [shaped((height, depth), BF16), shaped((width, width), BF16)],
        [
            pltpu.SMEM(tile_src.shape[2:], jnp.int32),
            pltpu.SMEM(tile_dst.shape[2:], jnp.int32),
            pltpu.VMEM(tiles.shape[2:], BF16),
            pltpu.VMEM(mask.shape, jnp.int32),
            pltpu.VMEM((width, width), BF16),
            pltpu.VMEM((height, depth), F32),
            pltpu.SemaphoreType.DMA((5,)),
        ],
        10_000_000,
        "build",
        True,
    )
    agg_flops = 2 * height * depth * width
    dense_flops = 2 * rows * width * width
    wide = shaped((rows, width), BF16)

    own_part, other_part = call(
        functools.partial(gather_kernel, 1 + rims),
        (matrix, state, *starts),
        [wide, wide],
        flops=agg_flops,
        name="gather",
    )
    received = swap_half(other_part)
    edge = call(
        edge_kernel, (count, state, own_part, received), [shaped((block, width), BF16)], name="edge"
    )[0]
    mixes = to_neighbours(edge, edge, edge, edge)
    x0, new, slope0 = call(
        forward_kernel,
        (count, state, own_part, received, masked0),
        [wide, wide, shaped((rows, width), F32)],
        flops=dense_flops,
        name="forward",
    )
    matrix_t, masked = call(
        later_kernel,
        (matrix, weights, mask),
        [shaped((depth, height), BF16), shaped((layers - 1, width, width), BF16)],
        flops=10_000_000,
        name="later",
    )
    own_part, other_part, slope_rim = call(
        functools.partial(rim_kernel, rims),
        (matrix, masked0, new, *starts, *mixes),
        [wide, wide, shaped((rims * block, width), F32)],
        flops=agg_flops + 2 * dense_flops,
        name="rim",
    )
    received = swap_half(other_part)
    x1, final, dz1, dx = call(
        last_kernel,
        (count, new, own_part, received, masked[0], cot),
        [wide, wide, wide, wide],
        flops=2 * dense_flops,
        name="last",
    )
    dx_other = swap_half(dx)
    final = call(emit_kernel, (final,), [wide], name="emit")[0]
    halves = [shaped((width, width // 2), F32), shaped((width, width // 2), BF16)]
    mine1, theirs1 = call(
        grad_kernel, (x1, dz1), halves, flops=dense_flops, name="grad"
    )
    share1 = phi_share(mine1, theirs1)
    xt = call(
        turn_kernel, (mine1, x0, *mixes), [shaped((width, depth), BF16)], flops=1_000_000, name="turn"
    )[0]
    mine0, theirs0 = call(
        back_kernel,
        (matrix_t, dx, dx_other, cot, slope0, slope_rim, xt),
        halves,
        flops=2 * agg_flops,
        name="back",
    )
    share0 = phi_share(mine0, theirs0)
    total1 = eta_sum(share1)
    other1 = swap_half(total1)
    total0 = eta_sum(share0)
    other0 = swap_half(total0)

    span = width // lax.axis_size("phi")
    row_ids = (lax.axis_index("phi") * span + jnp.arange(span, dtype=jnp.int32)) // side
    chosen = jnp.take(mask, row_ids, axis=1)
    keep = jnp.broadcast_to(chosen[..., None], (layers, span, grid, side)).reshape(
        layers, span, width
    )
    result = call(
        finish_kernel,
        (total0, other0, total1, other1, keep.astype(F32)),
        [shaped((layers, span, width), F32)],
        name="finish",
    )[0]
    return final[None, None], result


def solution(mesh):
    in_specs = (
        P(("group", "phi"), "eta", "half", None),
        P(("group", "phi"), "eta", "half", None),
        P(("group", "phi"), "eta", "half", None, None),
        P(("group", "phi"), "eta", "half"),
        P(("group", "phi"), "eta", "half"),
        P(),
        P(),
        P(("group", "phi"), "eta"),
    )
    out_specs = (P(("group", "phi"), "eta", "half", None), P("group", "phi", None))
    return jax.shard_map(body, mesh=mesh, in_specs=in_specs, out_specs=out_specs, check_vma=False)
```
